512 devices in a mesh: shard: 128 (over z, y, core), tensor: 4 (over x).
Axes of the slice: x: 4, y: 4, z: 16, core: 2. Of those that a mesh axis runs over, the one named last changes fastest.
Arguments:
- wo_grads: bfloat16 [4, 2, 8, 8, 512, 512], P('tensor', None, None, None, 'shard'), may hold values from -6 to 6
- wo_master: float32 [2, 8, 8, 512, 512], P(None, None, None, 'shard', 'tensor'), may hold values from -0.09375 to 0.09375
- left_stats: float32 [256, 512, 512], P('shard', 'tensor'), may hold values from -6 to 6
- right_stats: float32 [256, 512, 512], P('shard', 'tensor'), may hold values from -6 to 6
- left_roots: bfloat16 [256, 512, 512], P('shard', 'tensor'), as said below
- right_roots: bfloat16 [256, 512, 512], P('shard', 'tensor'), as said below
- row_moments: float32 [256, 512], P('shard'), may hold values from 0.003 to 0.05
- col_moments: float32 [256, 512], P('shard'), may hold values from 0.002 to 0.1
- owners: int32 [128], replicated, may hold values from 0 to 127, as said below
- emb_grads: bfloat16 [4, 4096, 4096], P('tensor', 'shard'), may hold values from -3 to 3
- emb_master: float32 [4096, 4096], P('shard', 'tensor'), may hold values from -0.75 to 0.75
- emb_mean: float32 [4096, 4096], P('shard', 'tensor'), may hold values from -0.75 to 0.75
- emb_var: float32 [4096, 4096], P('shard', 'tensor'), may hold values from 0.002 to 0.05
- gain_grads: bfloat16 [4, 2, 4096], P('tensor', None, 'shard'), may hold values from -3 to 3
- gain_master: float32 [2, 4096], P(None, ('shard', 'tensor')), may hold values from 0.5 to 1.5
- gain_mean: float32 [2, 4096], P(None, ('shard', 'tensor')), may hold values from -0.75 to 0.75
- gain_var: float32 [2, 4096], P(None, ('shard', 'tensor')), may hold values from 0.002 to 0.05
Outputs:
- wo_new: float32 [2, 8, 8, 512, 512], P(None, None, None, 'shard', 'tensor')
- wo_weights: bfloat16 [2, 8, 8, 512, 512], P(None, None, None, 'shard')
- left_new: float32 [256, 512, 512], P('shard', 'tensor')
- right_new: float32 [256, 512, 512], P('shard', 'tensor')
- row_new: float32 [256, 512], P('shard')
- col_new: float32 [256, 512], P('shard')
- emb_new: float32 [4096, 4096], P('shard', 'tensor')
- emb_mean_new: float32 [4096, 4096], P('shard', 'tensor')
- emb_var_new: float32 [4096, 4096], P('shard', 'tensor')
- emb_weights: bfloat16 [4096, 4096], P('shard')
- gain_new: float32 [2, 4096], P(None, ('shard', 'tensor'))
- gain_mean_new: float32 [2, 4096], P(None, ('shard', 'tensor'))
- gain_var_new: float32 [2, 4096], P(None, ('shard', 'tensor'))
- gain_weights: bfloat16 [2, 4096], P(None, 'shard')
The draws below stay inside these ranges and needn't reach their ends.
Inputs may be any that keep to these rules, and one draw needn't show every extreme that they name: `owners`: each index of shard owns at most 2 of the 128 blocks, and some index owns exactly 2. `left_roots`: each slot's matrix is symmetric. `right_roots`: each slot's matrix is symmetric.
All inputs are finite; a program needn't handle non-finite values.
Results may differ from the reference program's by a relative error of at most 0.0052.
Values may be sent and summed in bfloat16 or wider, within the bound.
No kernel may reach another device: no remote copies, remote signals or barrier semaphores. Data moves between devices by JAX's collectives and lax.ppermute only.
A program may use at most 128 MiB of HBM per device.

```python
import math
import jax
import jax.numpy as jnp
from jax import lax

D = 4096
MATS = 2
BLK = 512
MICRO = 4
NB = 8
NBLK = 128
SLOTS = 2
SLOTS_ALL = 256
EMB_ROWS = 4096
N_SHARD = 128


def draw_owners(key, part):
    slot_total = N_SHARD * SLOTS
    key_pick, key_rank, key_mix = jax.random.split(key, 3)
    chosen = jax.random.randint(key_pick, (), 0, N_SHARD)
    shuffle_rank = jax.random.permutation(key_rank, slot_total)
    slot_ids = jnp.arange(slot_total, dtype=jnp.int32)
    order_score = shuffle_rank + slot_total * (slot_ids // SLOTS != chosen).astype(jnp.int32)
    sorted_ids = jnp.argsort(order_score, stable=True)
    picked = jax.random.permutation(key_mix, sorted_ids[:NBLK])
    return (picked // SLOTS).astype(jnp.int32)


def draw_wo_grads(key, part):
    key_noise, key_rough = jax.random.split(jax.random.fold_in(key, 31))
    column = jnp.arange(BLK, dtype=jnp.float32) / (BLK - 1)
    rough = jnp.exp(jax.random.uniform(key_rough, (MATS, NB, NB, 1, BLK), jnp.float32, math.log(0.7), math.log(1.4)))
    noise = jax.random.normal(key_noise, (MICRO, MATS, NB, NB, BLK, BLK), jnp.float32)
    ramp = 0.05 * jnp.exp(column * math.log(20.0))
    values = noise * (ramp * rough)[None]
    return jnp.clip(values, -6.0, 6.0).astype(jnp.bfloat16)


def draw_col_moments(key, part):
    column = jnp.arange(BLK, dtype=jnp.float32) / (BLK - 1)
    rough = jnp.exp(jax.random.uniform(jax.random.fold_in(key, 47), (SLOTS_ALL, BLK), jnp.float32, math.log(0.7), math.log(1.4)))
    ramp = 0.005 * jnp.exp(column * math.log(10.0))
    return ramp[None, :] * rough


def symmetric_root(key):
    key_noise, key_diag = jax.random.split(key)
    noise_part = jax.random.normal(key_noise, (SLOTS_ALL, BLK, BLK), jnp.float32) * (0.7 / math.sqrt(BLK))
    diagonal = jnp.exp(jax.random.uniform(key_diag, (SLOTS_ALL, BLK), jnp.float32, math.log(0.5), math.log(2.0)))
    symmetric = 0.5 * (noise_part + jnp.swapaxes(noise_part, 1, 2))
    eye_mask = (jnp.arange(BLK)[:, None] == jnp.arange(BLK)[None, :]).astype(jnp.float32)
    return (symmetric * (1.0 - eye_mask) + diagonal[:, :, None] * eye_mask).astype(jnp.bfloat16)


def draw_left_roots(key, part):
    return symmetric_root(jax.random.fold_in(key, 11))


def draw_right_roots(key, part):
    return symmetric_root(jax.random.fold_in(key, 23))


def block_levels(key, extent, pieces, smallest, largest):
    gain, own = 1.0, jax.random.fold_in(key, 6)
    for dim, shards_of in pieces:
        draws = jnp.exp(jax.random.uniform(jax.random.fold_in(own, dim), (shards_of,), jnp.float32, smallest / len(pieces), largest / len(pieces)))
        gain = gain * jnp.repeat(draws, extent[dim] // shards_of).reshape([-1 if axis == dim else 1 for axis in range(len(extent))])
    return gain


def gaussian(key, dims, deviation, limit, cuts=(), held_as=jnp.bfloat16):
    result = jax.random.normal(key, dims, jnp.float32) * deviation
    if len(cuts) > 0:
        result = block_levels(key, dims, cuts, -0.22, 0.18) * result
    return jnp.clip(result, min=-limit, max=limit).astype(held_as)


def setup_inputs(seed: int = 0) -> dict:
    arg_keys = jax.random.split(jax.random.key(seed), 18)
    return {
        "wo_grads": draw_wo_grads(jax.random.fold_in(arg_keys[17], 71), 0),
        "wo_master": gaussian(arg_keys[1], (MATS, NB, NB, BLK, BLK), D ** -0.5, 0.09375, ((3, 128), (4, 4)), jnp.float32),
        "left_stats": gaussian(arg_keys[2], (SLOTS_ALL, BLK, BLK), 1.0, 6.0, ((0, 128), (1, 4)), jnp.float32),
        "right_stats": gaussian(arg_keys[3], (SLOTS_ALL, BLK, BLK), 1.0, 6.0, ((0, 128), (1, 4)), jnp.float32),
        "left_roots": draw_left_roots(jax.random.fold_in(arg_keys[17], 71), 0),
        "right_roots": draw_right_roots(jax.random.fold_in(arg_keys[17], 71), 0),
        "row_moments": jnp.clip(jnp.exp(math.log(0.05) - 2.8134107 * jax.random.uniform(arg_keys[6], (SLOTS_ALL, BLK), jnp.float32) ** block_levels(arg_keys[6], (SLOTS_ALL, BLK), ((0, 128),), -0.2, 0.2)), 0.003, 0.05),
        "col_moments": draw_col_moments(jax.random.fold_in(arg_keys[17], 71), 0),
        "owners": draw_owners(jax.random.fold_in(arg_keys[17], 71), 0),
        "emb_grads": gaussian(arg_keys[9], (MICRO, EMB_ROWS, D), 0.2, 3.0, ((0, 4), (1, 128))),
        "emb_master": gaussian(arg_keys[10], (EMB_ROWS, D), 0.05, 0.75, ((0, 128), (1, 4)), jnp.float32),
        "emb_mean": gaussian(arg_keys[11], (EMB_ROWS, D), 0.05, 0.75, ((0, 128), (1, 4)), jnp.float32),
        "emb_var": jnp.clip(jnp.exp(math.log(0.05) - 3.218876 * jax.random.uniform(arg_keys[12], (EMB_ROWS, D), jnp.float32) ** block_levels(arg_keys[12], (EMB_ROWS, D), ((0, 128), (1, 4)), -0.2, 0.2)), 0.002, 0.05),
        "gain_grads": gaussian(arg_keys[13], (MICRO, 2, D), 0.2, 3.0, ((0, 4), (2, 128))),
        "gain_master": jnp.clip(1.0 + 0.1 * jax.random.normal(arg_keys[14], (2, D), jnp.float32), 0.5, 1.5),
        "gain_mean": gaussian(arg_keys[15], (2, D), 0.05, 0.75, ((1, 512),), jnp.float32),
        "gain_var": jnp.clip(jnp.exp(math.log(0.05) - 3.218876 * jax.random.uniform(arg_keys[16], (2, D), jnp.float32) ** block_levels(arg_keys[16], (2, D), ((1, 512),), -0.2, 0.2)), 0.002, 0.05),
    }


beta_one = 0.9
beta_two = 0.95
bias_one = 1.0 - 0.9 ** 10
bias_two = 1.0 - 0.95 ** 10
adam_eps = 1e-08
learn_rate = 0.01
decay_rate = 0.1
graft_eps = 1e-06
factor_eps = 1e-08
highest = lax.Precision.HIGHEST

def slot_table(owners):
    block_ids = jnp.arange(owners.shape[0], dtype=jnp.int32)
    earlier = (owners[:, None] == owners[None, :]) & (block_ids[None, :] < block_ids[:, None])
    owner_rank = lax.optimization_barrier(jnp.sum(earlier.astype(jnp.int32), axis=1))
    slot_of = owners * SLOTS + owner_rank
    slot_ids = jnp.arange(SLOTS * N_SHARD, dtype=jnp.int32)
    slot_hits = (slot_of[:, None] == slot_ids[None, :]).astype(jnp.int32)
    block_of = lax.optimization_barrier(jnp.sum(slot_hits * block_ids[:, None], axis=0))
    slot_used = lax.optimization_barrier(jnp.sum(slot_hits, axis=0))
    return (slot_of, block_of, slot_used)

def adamw_step(gradient, master, first_moment, second_moment):
    mean_new = beta_one * first_moment + (1.0 - beta_one) * gradient
    var_new = beta_two * second_moment + (1.0 - beta_two) * gradient * gradient
    adam_dir = mean_new / bias_one / (jnp.sqrt(var_new / bias_two) + adam_eps)
    master_new = master - learn_rate * (adam_dir + decay_rate * master)
    return (master_new, mean_new, var_new, master_new.astype(jnp.bfloat16))

def shampoo_slot(slot_pack):
    gradient, left_stat, right_stat, left_root, right_root, row_state, col_state, slot_used = slot_pack
    squares = gradient * gradient
    row_new = beta_two * row_state + (1.0 - beta_two) * lax.optimization_barrier(jnp.mean(squares, axis=1))
    col_new = beta_two * col_state + (1.0 - beta_two) * lax.optimization_barrier(jnp.mean(squares, axis=0))

    def busy_slot(unused):
        left_new = left_stat + jnp.dot(gradient, gradient.T, precision=highest)
        right_new = right_stat + jnp.dot(gradient.T, gradient, precision=highest)
        second_est = row_new[:, None] * col_new[None, :] / jnp.mean(row_new)
        adam_dir = gradient / (jnp.sqrt(second_est) + factor_eps)
        right_half = jnp.dot(gradient.astype(jnp.bfloat16), right_root, preferred_element_type=jnp.float32).astype(jnp.bfloat16)
        shampoo = jnp.dot(left_root, right_half, preferred_element_type=jnp.float32)
        graft_ratio = jnp.sqrt(jnp.sum(adam_dir * adam_dir)) / (jnp.sqrt(jnp.sum(shampoo * shampoo)) + graft_eps)
        return (left_new, right_new, shampoo * graft_ratio)

    def empty_slot(unused):
        return (left_stat, right_stat, jnp.zeros_like(gradient))
    left_new, right_new, update = lax.cond(slot_used > 0, busy_slot, empty_slot, 0)
    return (left_new, right_new, row_new, col_new, update)

def reference(wo_grads, wo_master, left_stats, right_stats, left_roots, right_roots, row_moments, col_moments, owners, emb_grads, emb_master, emb_mean, emb_var, gain_grads, gain_master, gain_mean, gain_var):
    slot_of, block_of, slot_used = slot_table(owners)
    grad_mean = lax.optimization_barrier(jnp.sum(wo_grads.astype(jnp.float32), axis=0)) / MICRO
    flattened = grad_mean.reshape(NBLK, BLK, BLK)
    slot_grads = jnp.where(slot_used[:, None, None] > 0, flattened[block_of], 0.0)
    left_new, right_new, row_new, col_new, updates = lax.map(shampoo_slot, (slot_grads, left_stats, right_stats, left_roots, right_roots, row_moments, col_moments, slot_used))
    block_updates = updates[slot_of].reshape(MATS, NB, NB, BLK, BLK)
    wo_new = wo_master - learn_rate * (block_updates + decay_rate * wo_master)
    emb_grad = lax.optimization_barrier(jnp.sum(emb_grads.astype(jnp.float32), axis=0)) / MICRO
    gain_grad = lax.optimization_barrier(jnp.sum(gain_grads.astype(jnp.float32), axis=0)) / MICRO
    emb_new, emb_mean_new, emb_var_new, emb_weights = adamw_step(emb_grad, emb_master, emb_mean, emb_var)
    gain_new, gain_mean_new, gain_var_new, gain_weights = adamw_step(gain_grad, gain_master, gain_mean, gain_var)
    return (wo_new, wo_new.astype(jnp.bfloat16), left_new, right_new, row_new, col_new, emb_new, emb_mean_new, emb_var_new, emb_weights, gain_new, gain_mean_new, gain_var_new, gain_weights)
```

```python
import functools

import jax
import jax.numpy as jnp
from jax import lax
from jax.experimental import pallas as pl
from jax.experimental.pallas import tpu as pltpu
from jax.sharding import PartitionSpec as P


beta_one = 0.9
beta_two = 0.95
bias_one = 1.0 - 0.9**10
bias_two = 1.0 - 0.95**10
adam_eps = 1e-08
learn_rate = 0.01
decay_rate = 0.1
graft_eps = 1e-06
factor_eps = 1e-08
low = jnp.bfloat16
full = jnp.float32


def adamw_step(gradient, master, first_moment, second_moment):
    mean_new = beta_one * first_moment + (1.0 - beta_one) * gradient
    var_new = beta_two * second_moment + (1.0 - beta_two) * gradient * gradient
    adam_dir = mean_new / bias_one / (jnp.sqrt(var_new / bias_two) + adam_eps)
    master_new = master - learn_rate * (adam_dir + decay_rate * master)
    return (master_new, mean_new, var_new, master_new.astype(low))


def split_kernel(grads, parts):
    lanes = parts.shape[3]
    for member in range(parts.shape[0]):
        parts[member] = grads[:, :, member * lanes : (member + 1) * lanes]


def split_columns(grads, ways):
    blocks, rows, columns = grads.shape
    vmem = pl.BlockSpec(memory_space=pltpu.VMEM)
    return pl.pallas_call(
        split_kernel,
        out_shape=jax.ShapeDtypeStruct((ways, blocks, rows, columns // ways), grads.dtype),
        in_specs=[vmem],
        out_specs=vmem,
        name="split_columns",
    )(grads)


def place_kernel(slot_of, terms, slots):
    slots[...] = jnp.zeros_like(slots)
    micro_count, block_count = terms.shape[:2]

    def place(block, carry):
        total = terms[0, block].astype(full)
        for micro in range(1, micro_count):
            total = total + terms[micro, block].astype(full)
        slots[slot_of[block]] = (total / micro_count).astype(low)
        return carry

    lax.fori_loop(0, block_count, place, 0, unroll=8)


def place_blocks(slot_of, terms, slot_total):
    vmem = pl.BlockSpec(memory_space=pltpu.VMEM)
    return pl.pallas_call(
        place_kernel,
        out_shape=jax.ShapeDtypeStruct((slot_total,) + terms.shape[2:], low),
        in_specs=[pl.BlockSpec(memory_space=pltpu.SMEM), vmem],
        out_specs=vmem,
        name="place_blocks",
    )(slot_of, terms)


def core_kernel(here, columns, own, *rest, slot_count):
    ways = columns.shape[0]
    others, (row_old, col_old, update, row_new, col_new) = rest[: ways - 1], rest[ways - 1 :]
    factors = (own,) + tuple(others)
    quarter = own.shape[2]
    for slot in range(slot_count):
        block = jnp.concatenate([columns[member, slot] for member in range(ways)], axis=1)
        left = jnp.concatenate([factor[0, slot] for factor in factors], axis=0)
        right = jnp.concatenate([factor[1, slot] for factor in factors], axis=0)
        half = lax.dot_general(
            block, right, (((1,), (1,)), ((), ())), preferred_element_type=full
        ).astype(low)
        shampoo = jnp.dot(left, half, preferred_element_type=full)
        wide = block.astype(full)
        squares = wide * wide
        rows = beta_two * row_old[:, slot : slot + 1] + (1.0 - beta_two) * jnp.mean(
            squares, axis=1, keepdims=True
        )
        cols = beta_two * col_old[slot : slot + 1, :] + (1.0 - beta_two) * jnp.mean(
            squares, axis=0, keepdims=True
        )
        row_new[:, slot : slot + 1] = rows
        col_new[slot : slot + 1, :] = cols
        level = jnp.mean(rows, axis=0, keepdims=True)
        adam_dir = wide / (jnp.sqrt(rows) * jnp.sqrt(cols / level) + factor_eps)
        adam_total = jnp.sum(
            jnp.sum(adam_dir * adam_dir, axis=0, keepdims=True), axis=1, keepdims=True
        )
        shampoo_total = jnp.sum(
            jnp.sum(shampoo * shampoo, axis=0, keepdims=True), axis=1, keepdims=True
        )
        ratio = jnp.sqrt(adam_total) / (jnp.sqrt(shampoo_total) + graft_eps)
        for k in range(ways):
            member = lax.rem(here[0] - k + ways, ways)
            update[slot, pl.ds(member * quarter, quarter), :] = (
                shampoo[k * quarter : (k + 1) * quarter, :quarter] * ratio
            ).astype(low)


def precondition(here, columns, factors, row_old, col_old):
    _, slot_count, side, quarter = columns.shape
    vmem = pl.BlockSpec(memory_space=pltpu.VMEM)
    return pl.pallas_call(
        functools.partial(core_kernel, slot_count=slot_count),
        out_shape=(
            jax.ShapeDtypeStruct((slot_count, side, quarter), low),
            jax.ShapeDtypeStruct((side, slot_count), full),
            jax.ShapeDtypeStruct((slot_count, side), full),
        ),
        in_specs=[pl.BlockSpec(memory_space=pltpu.SMEM)] + [vmem] * (3 + len(factors)),
        out_specs=(vmem, vmem, vmem),
        name="precondition",
    )(here, columns, *factors, row_old, col_old)


def apply_kernel(slot_of, updates, master, master_new, weights):
    def step(block, carry):
        update = updates[slot_of[block]].astype(full)
        old = master[block]
        new = old - learn_rate * (update + decay_rate * old)
        master_new[block] = new
        rounded = new.astype(low)
        for copy in range(weights.shape[0]):
            weights[copy, block] = rounded
        return carry

    lax.fori_loop(0, master.shape[0], step, 0, unroll=8)


def apply_updates(slot_of, updates, master, copies):
    vmem = pl.BlockSpec(memory_space=pltpu.VMEM)
    return pl.pallas_call(
        apply_kernel,
        out_shape=(
            jax.ShapeDtypeStruct(master.shape, full),
            jax.ShapeDtypeStruct((copies,) + master.shape, low),
        ),
        in_specs=[pl.BlockSpec(memory_space=pltpu.SMEM), vmem, vmem],
        out_specs=(vmem, vmem),
        name="apply_updates",
    )(slot_of, updates, master)


def slots_of(owners, slot_count):
    ids = jnp.arange(owners.shape[0], dtype=jnp.int32)
    earlier = (owners[:, None] == owners[None, :]) & (ids[None, :] < ids[:, None])
    return owners * slot_count + jnp.sum(earlier.astype(jnp.int32), axis=1)


def in_order(pieces, position):
    count = len(pieces)
    turned = [pieces[(-j) % count] for j in range(count)]
    return lax.dynamic_slice_in_dim(
        jnp.stack(turned + turned), (count - position) % count, count, 0
    )


def from_peers(value_for, axis):
    count = lax.axis_size(axis)
    pieces = [value_for(0)]
    for k in range(1, count):
        value = value_for(k)
        pieces.append(lax.ppermute(value, axis, [(i, (i + k) % count) for i in range(count)]))
    return pieces


def per_device(
    wo_grads,
    wo_master,
    left_stats,
    right_stats,
    left_roots,
    right_roots,
    row_moments,
    col_moments,
    owners,
    emb_grads,
    emb_master,
    emb_mean,
    emb_var,
    gain_grads,
    gain_master,
    gain_mean,
    gain_var,
):
    ways = lax.axis_size("tensor")
    owner_count = lax.axis_size("shard")
    here = lax.axis_index("tensor")
    slot_count, quarter, side = left_stats.shape
    rows_dev = wo_master.shape[3]
    block_count = wo_master.shape[0] * wo_master.shape[1] * wo_master.shape[2]

    slot_of = slots_of(owners, slot_count)
    wo_parts = split_columns(wo_grads.reshape(block_count, rows_dev, side), ways)
    wo_terms = lax.all_to_all(wo_parts, "tensor", 0, 0, tiled=True)

    emb_rows, emb_cols = emb_master.shape
    gain_rows, gain_cols = gain_master.shape
    pad_rows = 8
    emb_parts = emb_grads[0].reshape(emb_rows, ways, emb_cols).transpose(1, 0, 2)
    gain_parts = gain_grads[0].reshape(gain_rows, ways, gain_cols).transpose(1, 0, 2)
    gain_parts = jnp.pad(
        gain_parts, ((0, 0), (0, pad_rows - gain_rows), (0, emb_cols - gain_cols))
    )
    small_parts = jnp.concatenate([emb_parts, gain_parts], axis=1)
    small_pieces = from_peers(
        lambda k: lax.dynamic_index_in_dim(small_parts, (here + k) % ways, 0, keepdims=False),
        "tensor",
    )
    small_sum = sum(piece.astype(full) for piece in small_pieces)

    outgoing = place_blocks(slot_of, wo_terms, owner_count * slot_count)
    outgoing = outgoing.reshape(owner_count, slot_count, rows_dev, quarter)
    own_cols = lax.all_to_all(outgoing, "shard", 0, 0, tiled=True)
    roots = jnp.stack([left_roots, right_roots])
    factors = from_peers(lambda k: roots, "tensor")

    own_cols, factors = lax.optimization_barrier((own_cols, factors))
    own_cols = own_cols.transpose(1, 0, 2, 3).reshape(slot_count, side, quarter)
    gathered = lax.all_to_all(
        jnp.broadcast_to(own_cols[None], (ways,) + own_cols.shape), "tensor", 0, 0, tiled=True
    )
    update, row_new, col_new = precondition(
        here.reshape(1).astype(jnp.int32), gathered, factors, row_moments.T, col_moments
    )
    row_new = row_new.T
    update = update.reshape(slot_count, owner_count, rows_dev, quarter).transpose(1, 0, 2, 3)
    returned = lax.all_to_all(update, "shard", 0, 0, tiled=True)

    block = gathered.transpose(1, 2, 0, 3).reshape(slot_count, side, side)
    own_rows = lax.dynamic_slice_in_dim(block, here * quarter, quarter, 1)
    left_new = left_stats + jnp.einsum("sqj,sij->sqi", own_rows, block, preferred_element_type=full)
    right_new = right_stats + jnp.einsum(
        "siq,sij->sqj", own_cols, block, preferred_element_type=full
    )

    small_grad = small_sum / ways
    emb_new, emb_mean_new, emb_var_new, emb_low = adamw_step(
        small_grad[:emb_rows], emb_master, emb_mean, emb_var
    )
    gain_new, gain_mean_new, gain_var_new, gain_low = adamw_step(
        small_grad[emb_rows : emb_rows + gain_rows, :gain_cols], gain_master, gain_mean, gain_var
    )
    gain_low = jnp.pad(gain_low, ((0, pad_rows - gain_rows), (0, emb_cols - gain_cols)))
    small_low = jnp.concatenate([emb_low, gain_low], axis=0)
    small_all = in_order(from_peers(lambda k: small_low, "tensor"), here)
    emb_weights = small_all[:, :emb_rows].transpose(1, 0, 2).reshape(emb_rows, ways * emb_cols)
    gain_weights = small_all[:, emb_rows : emb_rows + gain_rows, :gain_cols]
    gain_weights = gain_weights.transpose(1, 0, 2).reshape(gain_rows, ways * gain_cols)

    wo_new, wo_low = apply_updates(
        slot_of,
        returned.reshape(owner_count * slot_count, rows_dev, quarter),
        wo_master.reshape(block_count, rows_dev, quarter),
        ways,
    )
    wo_low = lax.all_to_all(wo_low, "tensor", 0, 0, tiled=True)
    wo_weights = wo_low.transpose(1, 2, 0, 3).reshape(wo_master.shape[:3] + (rows_dev, side))
    return (
        wo_new.reshape(wo_master.shape),
        wo_weights,
        left_new,
        right_new,
        row_new,
        col_new,
        emb_new,
        emb_mean_new,
        emb_var_new,
        emb_weights,
        gain_new,
        gain_mean_new,
        gain_var_new,
        gain_weights,
    )


def solution(mesh):
    in_specs = (
        P("tensor", None, None, None, "shard", None),
        P(None, None, None, "shard", "tensor"),
        P("shard", "tensor", None),
        P("shard", "tensor", None),
        P("shard", "tensor", None),
        P("shard", "tensor", None),
        P("shard", None),
        P("shard", None),
        P(),
        P("tensor", "shard", None),
        P("shard", "tensor"),
        P("shard", "tensor"),
        P("shard", "tensor"),
        P("tensor", None, "shard"),
        P(None, ("shard", "tensor")),
        P(None, ("shard", "tensor")),
        P(None, ("shard", "tensor")),
    )
    out_specs = (
        P(None, None, None, "shard", "tensor"),
        P(None, None, None, "shard", None),
        P("shard", "tensor", None),
        P("shard", "tensor", None),
        P("shard", None),
        P("shard", None),
        P("shard", "tensor"),
        P("shard", "tensor"),
        P("shard", "tensor"),
        P("shard", None),
        P(None, ("shard", "tensor")),
        P(None, ("shard", "tensor")),
        P(None, ("shard", "tensor")),
        P(None, "shard"),
    )

    return jax.shard_map(per_device, mesh=mesh, in_specs=in_specs, out_specs=out_specs, check_vma=False)
```

```python
import functools

import jax
import jax.numpy as jnp
from jax import lax
from jax.experimental import pallas as pl
from jax.experimental.pallas import tpu as pltpu
from jax.sharding import PartitionSpec as P


beta_one = 0.9
beta_two = 0.95
bias_one = 1.0 - 0.9**10
bias_two = 1.0 - 0.95**10
adam_eps = 1e-08
learn_rate = 0.01
decay_rate = 0.1
graft_eps = 1e-06
factor_eps = 1e-08
low = jnp.bfloat16
full = jnp.float32


def adamw_step(gradient, master, first_moment, second_moment):
    mean_new = beta_one * first_moment + (1.0 - beta_one) * gradient
    var_new = beta_two * second_moment + (1.0 - beta_two) * gradient * gradient
    adam_dir = mean_new / bias_one / (jnp.sqrt(var_new / bias_two) + adam_eps)
    master_new = master - learn_rate * (adam_dir + decay_rate * master)
    return (master_new, mean_new, var_new, master_new.astype(low))


def split_kernel(grads, parts):
    lanes = parts.shape[3]
    for member in range(parts.shape[0]):
        parts[member] = grads[:, :, member * lanes : (member + 1) * lanes]


def split_columns(grads, ways):
    blocks, rows, columns = grads.shape
    vmem = pl.BlockSpec(memory_space=pltpu.VMEM)
    return pl.pallas_call(
        split_kernel,
        out_shape=jax.ShapeDtypeStruct((ways, blocks, rows, columns // ways), grads.dtype),
        in_specs=[vmem],
        out_specs=vmem,
        name="split_columns",
    )(grads)


def place_kernel(slot_of, terms, slots):
    slots[...] = jnp.zeros_like(slots)
    micro_count, block_count = terms.shape[:2]

    def place(block, carry):
        total = terms[0, block].astype(full)
        for micro in range(1, micro_count):
            total = total + terms[micro, block].astype(full)
        slots[slot_of[block]] = (total / micro_count).astype(low)
        return carry

    lax.fori_loop(0, block_count, place, 0, unroll=8)


def place_blocks(slot_of, terms, slot_total):
    vmem = pl.BlockSpec(memory_space=pltpu.VMEM)
    return pl.pallas_call(
        place_kernel,
        out_shape=jax.ShapeDtypeStruct((slot_total,) + terms.shape[2:], low),
        in_specs=[pl.BlockSpec(memory_space=pltpu.SMEM), vmem],
        out_specs=vmem,
        name="place_blocks",
    )(slot_of, terms)


def core_kernel(here, columns, own, *rest, slot_count):
    ways = columns.shape[0]
    others, (row_old, col_old, update, row_new, col_new) = rest[: ways - 1], rest[ways - 1 :]
    factors = (own,) + tuple(others)
    quarter = own.shape[2]
    for slot in range(slot_count):
        block = jnp.concatenate([columns[member, slot] for member in range(ways)], axis=1)
        left = jnp.concatenate([factor[0, slot] for factor in factors], axis=0)
        right = jnp.concatenate([factor[1, slot] for factor in factors], axis=0)
        half = lax.dot_general(
            block, right, (((1,), (1,)), ((), ())), preferred_element_type=full
        ).astype(low)
        shampoo = jnp.dot(left, half, preferred_element_type=full)
        wide = block.astype(full)
        squares = wide * wide
        rows = beta_two * row_old[:, slot : slot + 1] + (1.0 - beta_two) * jnp.mean(
            squares, axis=1, keepdims=True
        )
        cols = beta_two * col_old[slot : slot + 1, :] + (1.0 - beta_two) * jnp.mean(
            squares, axis=0, keepdims=True
        )
        row_new[:, slot : slot + 1] = rows
        col_new[slot : slot + 1, :] = cols
        level = jnp.mean(rows, axis=0, keepdims=True)
        adam_dir = wide / (jnp.sqrt(rows) * jnp.sqrt(cols / level) + factor_eps)
        adam_total = jnp.sum(
            jnp.sum(adam_dir * adam_dir, axis=0, keepdims=True), axis=1, keepdims=True
        )
        shampoo_total = jnp.sum(
            jnp.sum(shampoo * shampoo, axis=0, keepdims=True), axis=1, keepdims=True
        )
        ratio = jnp.sqrt(adam_total) / (jnp.sqrt(shampoo_total) + graft_eps)
        for k in range(ways):
            member = lax.rem(here[0] - k + ways, ways)
            part = shampoo[k * quarter : (k + 1) * quarter, :quarter] * ratio
            owners_here = quarter // update.shape[2]
            update[pl.ds(member * owners_here, owners_here), slot] = part.reshape(
                owners_here, update.shape[2], quarter
            ).astype(low)


def precondition(here, columns, factors, row_old, col_old, rows_dev):
    _, slot_count, side, quarter = columns.shape
    vmem = pl.BlockSpec(memory_space=pltpu.VMEM)
    return pl.pallas_call(
        functools.partial(core_kernel, slot_count=slot_count),
        out_shape=(
            jax.ShapeDtypeStruct((side // rows_dev, slot_count, rows_dev, quarter), low),
            jax.ShapeDtypeStruct((side, slot_count), full),
            jax.ShapeDtypeStruct((slot_count, side), full),
        ),
        in_specs=[pl.BlockSpec(memory_space=pltpu.SMEM)] + [vmem] * (3 + len(factors)),
        out_specs=(vmem, vmem, vmem),
        name="precondition",
    )(here, columns, *factors, row_old, col_old)


def apply_kernel(slot_of, updates, master, master_new, weights):
    def step(block, carry):
        update = updates[slot_of[block]].astype(full)
        old = master[block]
        new = old - learn_rate * (update + decay_rate * old)
        master_new[block] = new
        rounded = new.astype(low)
        for copy in range(weights.shape[0]):
            weights[copy, block] = rounded
        return carry

    lax.fori_loop(0, master.shape[0], step, 0, unroll=8)


def apply_updates(slot_of, updates, master, copies):
    vmem = pl.BlockSpec(memory_space=pltpu.VMEM)
    return pl.pallas_call(
        apply_kernel,
        out_shape=(
            jax.ShapeDtypeStruct(master.shape, full),
            jax.ShapeDtypeStruct((copies,) + master.shape, low),
        ),
        in_specs=[pl.BlockSpec(memory_space=pltpu.SMEM), vmem, vmem],
        out_specs=(vmem, vmem),
        name="apply_updates",
    )(slot_of, updates, master)


def slots_of(owners, slot_count):
    ids = jnp.arange(owners.shape[0], dtype=jnp.int32)
    earlier = (owners[:, None] == owners[None, :]) & (ids[None, :] < ids[:, None])
    return owners * slot_count + jnp.sum(earlier.astype(jnp.int32), axis=1)


def in_order(pieces, position):
    count = len(pieces)
    turned = [pieces[(-j) % count] for j in range(count)]
    return lax.dynamic_slice_in_dim(
        jnp.stack(turned + turned), (count - position) % count, count, 0
    )


def from_peers(value_for, axis):
    count = lax.axis_size(axis)
    pieces = [value_for(0)]
    for k in range(1, count):
        value = value_for(k)
        pieces.append(lax.ppermute(value, axis, [(i, (i + k) % count) for i in range(count)]))
    return pieces


def per_device(
    wo_grads,
    wo_master,
    left_stats,
    right_stats,
    left_roots,
    right_roots,
    row_moments,
    col_moments,
    owners,
    emb_grads,
    emb_master,
    emb_mean,
    emb_var,
    gain_grads,
    gain_master,
    gain_mean,
    gain_var,
):
    ways = lax.axis_size("tensor")
    owner_count = lax.axis_size("shard")
    here = lax.axis_index("tensor")
    slot_count, quarter, side = left_stats.shape
    rows_dev = wo_master.shape[3]
    block_count = wo_master.shape[0] * wo_master.shape[1] * wo_master.shape[2]

    slot_of = slots_of(owners, slot_count)
    wo_parts = split_columns(wo_grads.reshape(block_count, rows_dev, side), ways)
    wo_terms = lax.all_to_all(wo_parts, "tensor", 0, 0, tiled=True)

    roots = jnp.stack([left_roots, right_roots])
    factors = from_peers(lambda k: roots, "tensor")

    emb_rows, emb_cols = emb_master.shape
    gain_rows, gain_cols = gain_master.shape
    pad_rows = 8
    emb_parts = emb_grads[0].reshape(emb_rows, ways, emb_cols).transpose(1, 0, 2)
    gain_parts = gain_grads[0].reshape(gain_rows, ways, gain_cols).transpose(1, 0, 2)
    gain_parts = jnp.pad(
        gain_parts, ((0, 0), (0, pad_rows - gain_rows), (0, emb_cols - gain_cols))
    )
    small_parts = jnp.concatenate([emb_parts, gain_parts], axis=1)
    small_pieces = from_peers(
        lambda k: lax.dynamic_index_in_dim(small_parts, (here + k) % ways, 0, keepdims=False),
        "tensor",
    )
    small_sum = sum(piece.astype(full) for piece in small_pieces)

    outgoing = place_blocks(slot_of, wo_terms, owner_count * slot_count)
    outgoing = outgoing.reshape(owner_count, slot_count, rows_dev, quarter)
    own_cols = lax.all_to_all(outgoing, "shard", 0, 0, tiled=True)
    own_cols, factors, small_sum = lax.optimization_barrier((own_cols, factors, small_sum))
    own_cols = own_cols.transpose(1, 0, 2, 3).reshape(slot_count, side, quarter)
    gathered = lax.all_to_all(
        jnp.broadcast_to(own_cols[None], (ways,) + own_cols.shape), "tensor", 0, 0, tiled=True
    )
    update, row_new, col_new = precondition(
        here.reshape(1).astype(jnp.int32), gathered, factors, row_moments.T, col_moments, rows_dev
    )
    row_new = row_new.T
    returned = lax.all_to_all(update, "shard", 0, 0, tiled=True)

    block = gathered.transpose(1, 2, 0, 3).reshape(slot_count, side, side)
    own_rows = lax.dynamic_slice_in_dim(block, here * quarter, quarter, 1)
    left_new = left_stats + jnp.einsum("sqj,sij->sqi", own_rows, block, preferred_element_type=full)
    right_new = right_stats + jnp.einsum(
        "siq,sij->sqj", own_cols, block, preferred_element_type=full
    )

    small_grad = small_sum / ways
    emb_new, emb_mean_new, emb_var_new, emb_low = adamw_step(
        small_grad[:emb_rows], emb_master, emb_mean, emb_var
    )
    gain_new, gain_mean_new, gain_var_new, gain_low = adamw_step(
        small_grad[emb_rows : emb_rows + gain_rows, :gain_cols], gain_master, gain_mean, gain_var
    )
    gain_low = jnp.pad(gain_low, ((0, pad_rows - gain_rows), (0, emb_cols - gain_cols)))
    small_low = jnp.concatenate([emb_low, gain_low], axis=0)
    small_all = in_order(from_peers(lambda k: small_low, "tensor"), here)
    emb_weights = small_all[:, :emb_rows].transpose(1, 0, 2).reshape(emb_rows, ways * emb_cols)
    gain_weights = small_all[:, emb_rows : emb_rows + gain_rows, :gain_cols]
    gain_weights = gain_weights.transpose(1, 0, 2).reshape(gain_rows, ways * gain_cols)

    wo_new, wo_low = apply_updates(
        slot_of,
        returned.reshape(owner_count * slot_count, rows_dev, quarter),
        wo_master.reshape(block_count, rows_dev, quarter),
        ways,
    )
    wo_low = lax.all_to_all(wo_low, "tensor", 0, 0, tiled=True)
    wo_weights = jnp.concatenate([wo_low[member] for member in range(ways)], axis=-1)
    wo_weights = wo_weights.reshape(wo_master.shape[:3] + (rows_dev, side))
    return (
        wo_new.reshape(wo_master.shape),
        wo_weights,
        left_new,
        right_new,
        row_new,
        col_new,
        emb_new,
        emb_mean_new,
        emb_var_new,
        emb_weights,
        gain_new,
        gain_mean_new,
        gain_var_new,
        gain_weights,
    )


def solution(mesh):
    in_specs = (
        P("tensor", None, None, None, "shard", None),
        P(None, None, None, "shard", "tensor"),
        P("shard", "tensor", None),
        P("shard", "tensor", None),
        P("shard", "tensor", None),
        P("shard", "tensor", None),
        P("shard", None),
        P("shard", None),
        P(),
        P("tensor", "shard", None),
        P("shard", "tensor"),
        P("shard", "tensor"),
        P("shard", "tensor"),
        P("tensor", None, "shard"),
        P(None, ("shard", "tensor")),
        P(None, ("shard", "tensor")),
        P(None, ("shard", "tensor")),
    )
    out_specs = (
        P(None, None, None, "shard", "tensor"),
        P(None, None, None, "shard", None),
        P("shard", "tensor", None),
        P("shard", "tensor", None),
        P("shard", None),
        P("shard", None),
        P("shard", "tensor"),
        P("shard", "tensor"),
        P("shard", "tensor"),
        P("shard", None),
        P(None, ("shard", "tensor")),
        P(None, ("shard", "tensor")),
        P(None, ("shard", "tensor")),
        P(None, "shard"),
    )

    return jax.shard_map(per_device, mesh=mesh, in_specs=in_specs, out_specs=out_specs, check_vma=False)
```

```python
import functools

import jax
import jax.numpy as jnp
from jax import lax
from jax.experimental import pallas as pl
from jax.experimental.pallas import tpu as pltpu
from jax.sharding import PartitionSpec as P


beta_one = 0.9
beta_two = 0.95
bias_one = 1.0 - 0.9**10
bias_two = 1.0 - 0.95**10
adam_eps = 1e-08
learn_rate = 0.01
decay_rate = 0.1
graft_eps = 1e-06
factor_eps = 1e-08
low = jnp.bfloat16
full = jnp.float32


def adamw_step(gradient, master, first_moment, second_moment):
    mean_new = beta_one * first_moment + (1.0 - beta_one) * gradient
    var_new = beta_two * second_moment + (1.0 - beta_two) * gradient * gradient
    adam_dir = mean_new / bias_one / (jnp.sqrt(var_new / bias_two) + adam_eps)
    master_new = master - learn_rate * (adam_dir + decay_rate * master)
    return (master_new, mean_new, var_new, master_new.astype(low))


def split_kernel(grads, parts):
    lanes = parts.shape[3]
    for member in range(parts.shape[0]):
        parts[member] = grads[:, :, member * lanes : (member + 1) * lanes]


def split_columns(grads, ways):
    blocks, rows, columns = grads.shape
    vmem = pl.BlockSpec(memory_space=pltpu.VMEM)
    return pl.pallas_call(
        split_kernel,
        out_shape=jax.ShapeDtypeStruct((ways, blocks, rows, columns // ways), grads.dtype),
        in_specs=[vmem],
        out_specs=vmem,
        name="split_columns",
    )(grads)


def place_kernel(slot_of, terms, slots):
    slots[...] = jnp.zeros_like(slots)
    micro_count, block_count = terms.shape[:2]

    def place(block, carry):
        total = terms[0, block].astype(full)
        for micro in range(1, micro_count):
            total = total + terms[micro, block].astype(full)
        slots[slot_of[block]] = (total / micro_count).astype(low)
        return carry

    lax.fori_loop(0, block_count, place, 0, unroll=8)


def place_blocks(slot_of, terms, slot_total):
    vmem = pl.BlockSpec(memory_space=pltpu.VMEM)
    return pl.pallas_call(
        place_kernel,
        out_shape=jax.ShapeDtypeStruct((slot_total,) + terms.shape[2:], low),
        in_specs=[pl.BlockSpec(memory_space=pltpu.SMEM), vmem],
        out_specs=vmem,
        name="place_blocks",
    )(slot_of, terms)


def core_kernel(here, columns, own, *rest, slot_count):
    ways = columns.shape[0]
    others, (row_old, col_old, update, row_new, col_new) = rest[: ways - 1], rest[ways - 1 :]
    factors = (own,) + tuple(others)
    quarter = own.shape[2]
    for slot in range(slot_count):
        block = jnp.concatenate([columns[member, slot] for member in range(ways)], axis=1)
        left = jnp.concatenate([factor[0, slot] for factor in factors], axis=0)
        right = jnp.concatenate([factor[1, slot] for factor in factors], axis=0)
        half = lax.dot_general(
            block, right, (((1,), (1,)), ((), ())), preferred_element_type=full
        ).astype(low)
        shampoo = jnp.dot(left, half, preferred_element_type=full)
        wide = block.astype(full)
        squares = wide * wide
        rows = beta_two * row_old[:, slot : slot + 1] + (1.0 - beta_two) * jnp.mean(
            squares, axis=1, keepdims=True
        )
        cols = beta_two * col_old[slot : slot + 1, :] + (1.0 - beta_two) * jnp.mean(
            squares, axis=0, keepdims=True
        )
        row_new[:, slot : slot + 1] = rows
        col_new[slot : slot + 1, :] = cols
        level = jnp.mean(rows, axis=0, keepdims=True)
        adam_dir = wide / (jnp.sqrt(rows) * jnp.sqrt(cols / level) + factor_eps)
        adam_total = jnp.sum(
            jnp.sum(adam_dir * adam_dir, axis=0, keepdims=True), axis=1, keepdims=True
        )
        shampoo_total = jnp.sum(
            jnp.sum(shampoo * shampoo, axis=0, keepdims=True), axis=1, keepdims=True
        )
        ratio = jnp.sqrt(adam_total) / (jnp.sqrt(shampoo_total) + graft_eps)
        for k in range(ways):
            member = lax.rem(here[0] - k + ways, ways)
            part = shampoo[k * quarter : (k + 1) * quarter, :quarter] * ratio
            owners_here = quarter // update.shape[2]
            update[pl.ds(member * owners_here, owners_here), slot] = part.reshape(
                owners_here, update.shape[2], quarter
            ).astype(low)


def precondition(here, columns, factors, row_old, col_old, rows_dev):
    _, slot_count, side, quarter = columns.shape
    vmem = pl.BlockSpec(memory_space=pltpu.VMEM)
    return pl.pallas_call(
        functools.partial(core_kernel, slot_count=slot_count),
        out_shape=(
            jax.ShapeDtypeStruct((side // rows_dev, slot_count, rows_dev, quarter), low),
            jax.ShapeDtypeStruct((side, slot_count), full),
            jax.ShapeDtypeStruct((slot_count, side), full),
        ),
        in_specs=[pl.BlockSpec(memory_space=pltpu.SMEM)] + [vmem] * (3 + len(factors)),
        out_specs=(vmem, vmem, vmem),
        name="precondition",
    )(here, columns, *factors, row_old, col_old)


def apply_kernel(slot_of, updates, master, master_new, weights):
    def step(block, carry):
        update = updates[slot_of[block]].astype(full)
        old = master[block]
        new = old - learn_rate * (update + decay_rate * old)
        master_new[block] = new
        rounded = new.astype(low)
        for copy in range(weights.shape[0]):
            weights[copy, block] = rounded
        return carry

    lax.fori_loop(0, master.shape[0], step, 0, unroll=8)


def apply_updates(slot_of, updates, master, copies):
    vmem = pl.BlockSpec(memory_space=pltpu.VMEM)
    return pl.pallas_call(
        apply_kernel,
        out_shape=(
            jax.ShapeDtypeStruct(master.shape, full),
            jax.ShapeDtypeStruct((copies,) + master.shape, low),
        ),
        in_specs=[pl.BlockSpec(memory_space=pltpu.SMEM), vmem, vmem],
        out_specs=(vmem, vmem),
        name="apply_updates",
    )(slot_of, updates, master)


def in_vmem(value):
    return pltpu.with_memory_space_constraint(value, pltpu.VMEM)


def slots_of(owners, slot_count):
    ids = jnp.arange(owners.shape[0], dtype=jnp.int32)
    earlier = (owners[:, None] == owners[None, :]) & (ids[None, :] < ids[:, None])
    return owners * slot_count + jnp.sum(earlier.astype(jnp.int32), axis=1)


def in_order(pieces, position):
    count = len(pieces)
    turned = [pieces[(-j) % count] for j in range(count)]
    return lax.dynamic_slice_in_dim(
        jnp.stack(turned + turned), (count - position) % count, count, 0
    )


def from_peers(value_for, axis):
    count = lax.axis_size(axis)
    pieces = [value_for(0)]
    for k in range(1, count):
        value = value_for(k)
        pieces.append(lax.ppermute(value, axis, [(i, (i + k) % count) for i in range(count)]))
    return pieces


def per_device(
    wo_grads,
    wo_master,
    left_stats,
    right_stats,
    left_roots,
    right_roots,
    row_moments,
    col_moments,
    owners,
    emb_grads,
    emb_master,
    emb_mean,
    emb_var,
    gain_grads,
    gain_master,
    gain_mean,
    gain_var,
):
    ways = lax.axis_size("tensor")
    owner_count = lax.axis_size("shard")
    here = lax.axis_index("tensor")
    slot_count, quarter, side = left_stats.shape
    rows_dev = wo_master.shape[3]
    block_count = wo_master.shape[0] * wo_master.shape[1] * wo_master.shape[2]

    slot_of = slots_of(owners, slot_count)
    wo_parts = split_columns(wo_grads.reshape(block_count, rows_dev, side), ways)
    wo_terms = lax.all_to_all(wo_parts, "tensor", 0, 0, tiled=True)

    roots = jnp.stack([left_roots, right_roots])
    factors = from_peers(lambda k: roots, "tensor")

    emb_rows, emb_cols = emb_master.shape
    gain_rows, gain_cols = gain_master.shape
    pad_rows = 8
    emb_parts = emb_grads[0].reshape(emb_rows, ways, emb_cols).transpose(1, 0, 2)
    gain_parts = gain_grads[0].reshape(gain_rows, ways, gain_cols).transpose(1, 0, 2)
    gain_parts = jnp.pad(
        gain_parts, ((0, 0), (0, pad_rows - gain_rows), (0, emb_cols - gain_cols))
    )
    small_parts = jnp.concatenate([emb_parts, gain_parts], axis=1)
    small_pieces = from_peers(
        lambda k: lax.dynamic_index_in_dim(small_parts, (here + k) % ways, 0, keepdims=False),
        "tensor",
    )
    small_sum = sum(piece.astype(full) for piece in small_pieces)

    outgoing = place_blocks(slot_of, in_vmem(wo_terms), owner_count * slot_count)
    outgoing = outgoing.reshape(owner_count, slot_count, rows_dev, quarter)
    own_cols = lax.all_to_all(outgoing, "shard", 0, 0, tiled=True)
    own_cols, factors = lax.optimization_barrier((own_cols, factors))
    own_cols = own_cols.transpose(1, 0, 2, 3).reshape(slot_count, side, quarter)
    gathered = lax.all_to_all(
        jnp.broadcast_to(own_cols[None], (ways,) + own_cols.shape), "tensor", 0, 0, tiled=True
    )
    update, row_new, col_new = precondition(
        here.reshape(1).astype(jnp.int32), in_vmem(gathered), factors, row_moments.T, col_moments, rows_dev
    )
    row_new = row_new.T
    returned = lax.all_to_all(update, "shard", 0, 0, tiled=True)

    block = gathered.transpose(1, 2, 0, 3).reshape(slot_count, side, side)
    own_rows = lax.dynamic_slice_in_dim(block, here * quarter, quarter, 1)
    left_new = left_stats + jnp.einsum("sqj,sij->sqi", own_rows, block, preferred_element_type=full)
    right_new = right_stats + jnp.einsum(
        "siq,sij->sqj", own_cols, block, preferred_element_type=full
    )

    small_grad = small_sum / ways
    emb_new, emb_mean_new, emb_var_new, emb_low = adamw_step(
        small_grad[:emb_rows], emb_master, emb_mean, emb_var
    )
    gain_new, gain_mean_new, gain_var_new, gain_low = adamw_step(
        small_grad[emb_rows : emb_rows + gain_rows, :gain_cols], gain_master, gain_mean, gain_var
    )
    gain_low = jnp.pad(gain_low, ((0, pad_rows - gain_rows), (0, emb_cols - gain_cols)))
    small_low = jnp.concatenate([emb_low, gain_low], axis=0)
    small_all = in_order(from_peers(lambda k: small_low, "tensor"), here)
    emb_weights = small_all[:, :emb_rows].transpose(1, 0, 2).reshape(emb_rows, ways * emb_cols)
    gain_weights = small_all[:, emb_rows : emb_rows + gain_rows, :gain_cols]
    gain_weights = gain_weights.transpose(1, 0, 2).reshape(gain_rows, ways * gain_cols)

    wo_new, wo_low = apply_updates(
        slot_of,
        in_vmem(returned.reshape(owner_count * slot_count, rows_dev, quarter)),
        wo_master.reshape(block_count, rows_dev, quarter),
        ways,
    )
    wo_low = lax.all_to_all(wo_low, "tensor", 0, 0, tiled=True)
    wo_weights = jnp.concatenate([wo_low[member] for member in range(ways)], axis=-1)
    wo_weights = wo_weights.reshape(wo_master.shape[:3] + (rows_dev, side))
    return (
        wo_new.reshape(wo_master.shape),
        wo_weights,
        left_new,
        right_new,
        row_new,
        col_new,
        emb_new,
        emb_mean_new,
        emb_var_new,
        emb_weights,
        gain_new,
        gain_mean_new,
        gain_var_new,
        gain_weights,
    )


def solution(mesh):
    in_specs = (
        P("tensor", None, None, None, "shard", None),
        P(None, None, None, "shard", "tensor"),
        P("shard", "tensor", None),
        P("shard", "tensor", None),
        P("shard", "tensor", None),
        P("shard", "tensor", None),
        P("shard", None),
        P("shard", None),
        P(),
        P("tensor", "shard", None),
        P("shard", "tensor"),
        P("shard", "tensor"),
        P("shard", "tensor"),
        P("tensor", None, "shard"),
        P(None, ("shard", "tensor")),
        P(None, ("shard", "tensor")),
        P(None, ("shard", "tensor")),
    )
    out_specs = (
        P(None, None, None, "shard", "tensor"),
        P(None, None, None, "shard", None),
        P("shard", "tensor", None),
        P("shard", "tensor", None),
        P("shard", None),
        P("shard", None),
        P("shard", "tensor"),
        P("shard", "tensor"),
        P("shard", "tensor"),
        P("shard", None),
        P(None, ("shard", "tensor")),
        P(None, ("shard", "tensor")),
        P(None, ("shard", "tensor")),
        P(None, "shard"),
    )

    return jax.shard_map(per_device, mesh=mesh, in_specs=in_specs, out_specs=out_specs, check_vma=False)
```
